256 devices in a mesh: heads: 8 (over x, core), ctx: 32 (over z, y).
Axes of the slice: x: 4, y: 4, z: 8, core: 2. Of those that a mesh axis runs over, the one named last changes fastest.
Arguments:
- queries: bfloat16 [8192, 4096], P('ctx', 'heads'), may hold values from -5 to 5
- key_rows: bfloat16 [8192, 4096], P('ctx', 'heads'), may hold values from -5 to 5
- value_rows: bfloat16 [8192, 4096], P('ctx', 'heads'), may hold values from -6 to 6
- log_decay: float32 [8192, 32], P('ctx', 'heads'), may hold values from -1 to 0
- write_rate: float32 [8192, 32], P('ctx', 'heads'), may hold values from 0 to 1
- block_list: int32 [128, 4], P('ctx'), may hold values from 0 to 127, as said below
- attn_gain: float32 [4096], P('heads'), may hold values from 0.1 to 1.9
- delta_gain: float32 [4096], P('heads'), may hold values from 0.1 to 1.9
- out_weight: bfloat16 [4096, 4096], P('heads'), may hold values from -0.09375 to 0.09375
Outputs:
- layer_out: bfloat16 [8192, 4096], P(('ctx', 'heads'))
The draws below stay inside these ranges and needn't reach their ends.
Inputs may be any that keep to these rules, and one draw needn't show every extreme that they name: `block_list`: entry 0 of query block i's list is i itself. Of the other entries of the 4 query blocks of one shard of 256 tokens, at most 2 name key blocks of any one shard; in every draw some shard is named exactly 2 times by the other entries of every shard.
All inputs are finite; a program needn't handle non-finite values.
Results may differ from the reference program's by a relative error of at most 0.014.
Values may be sent and summed in bfloat16 or wider, within the bound.
No kernel may reach another device: no remote copies, remote signals or barrier semaphores. Data moves between devices by JAX's collectives and lax.ppermute only.
A program may use at most 64 MiB of HBM per device.

```python
import math
import jax
import jax.numpy as jnp
from jax import lax

D = 4096
HEAD_COUNT = 32
HDIM = 128
L_DEV = 256
BLK = 64
NSEL = 4
GROUPS = 8
SHARDS = 32
TOKEN_COUNT = 8192
QB_DEV = 4
NQB = 128
CAP = 2


def paired_rows(key):
    random_base_key = jax.random.fold_in(key, 101)
    column_scales = jnp.exp(jax.random.uniform(jax.random.fold_in(random_base_key, 8), (D,), jnp.float32, math.log(0.2), math.log(2.5)))
    query_vals = jnp.clip(jax.random.normal(jax.random.fold_in(random_base_key, 5), (TOKEN_COUNT, D), jnp.float32), -5.0, 5.0)
    key_vals = jnp.clip(jax.random.normal(jax.random.fold_in(random_base_key, 6), (TOKEN_COUNT, D), jnp.float32) * column_scales[None, :], -5.0, 5.0)
    return (query_vals, key_vals)


def draw_queries(key, part):
    return paired_rows(key)[0].astype(jnp.bfloat16)


def draw_key_rows(key, part):
    return paired_rows(key)[1].astype(jnp.bfloat16)


def head_profile(key):
    random_base_key = jax.random.fold_in(key, 202)
    slow_share = 0.5
    slow_heads = jax.random.bernoulli(jax.random.fold_in(random_base_key, 1), slow_share, (HEAD_COUNT,))
    return (slow_heads, random_base_key)


def draw_log_decay(key, part):
    slow_heads, random_base_key = head_profile(key)
    fast_rate = jnp.exp(jax.random.uniform(jax.random.fold_in(random_base_key, 2), (HEAD_COUNT,), jnp.float32, math.log(1.0 / 50.0), math.log(1.0 / 30.0)))
    slow_rate = jnp.exp(jax.random.uniform(jax.random.fold_in(random_base_key, 3), (HEAD_COUNT,), jnp.float32, math.log(0.02), math.log(0.3))) / TOKEN_COUNT
    base_rate = jnp.where(slow_heads, slow_rate, fast_rate)
    shard_factor = jnp.exp(jax.random.uniform(jax.random.fold_in(random_base_key, 4), (SHARDS, HEAD_COUNT), jnp.float32, math.log(0.5), math.log(2.0)))
    token_factor = jax.random.uniform(jax.random.fold_in(random_base_key, 5), (TOKEN_COUNT, HEAD_COUNT), jnp.float32, 0.5, 1.5)
    rates = base_rate[None, :] * jnp.repeat(shard_factor, L_DEV, axis=0) * token_factor
    surge_rows = jax.random.randint(jax.random.fold_in(random_base_key, 6), (2, HEAD_COUNT), 0, TOKEN_COUNT)
    surge_depth = jnp.log(jax.random.uniform(jax.random.fold_in(random_base_key, 7), (2, HEAD_COUNT), jnp.float32, 0.55, 0.8))
    head_columns = jnp.broadcast_to(jnp.arange(HEAD_COUNT)[None, :], (2, HEAD_COUNT))
    dropped_entries = jnp.zeros((TOKEN_COUNT, HEAD_COUNT), jnp.float32).at[surge_rows, head_columns].add(surge_depth)
    return -rates + dropped_entries


def draw_write_rate(key, part):
    slow_heads, random_base_key = head_profile(key)
    fast_vals = jax.random.uniform(jax.random.fold_in(random_base_key, 8), (TOKEN_COUNT, HEAD_COUNT), jnp.float32, 0.2, 0.9)
    slow_vals = jax.random.uniform(jax.random.fold_in(random_base_key, 9), (TOKEN_COUNT, HEAD_COUNT), jnp.float32, 0.2, 0.9)
    return jnp.where(slow_heads[None, :], slow_vals, fast_vals)


def draw_block_list(key, part):
    random_base_key = jax.random.fold_in(key, 303)
    pairs = SHARDS * CAP
    requests = QB_DEV * (NSEL - 1)
    favored = jax.random.randint(jax.random.fold_in(random_base_key, 1), (), 0, SHARDS)

    def one_shard(shard):
        shard_key = jax.random.fold_in(random_base_key, 1000 + shard)
        boost = jax.random.randint(jax.random.fold_in(shard_key, 1), (SHARDS,), 0, 1024)
        boost = boost + jnp.where(jnp.arange(SHARDS) == favored, 2048, 0)
        pair_owner = jnp.arange(pairs) // CAP
        noise = jax.random.randint(jax.random.fold_in(shard_key, 2), (pairs,), 0, 1024)
        score = (boost[pair_owner] * 1024 + noise) * pairs + jnp.arange(pairs)
        _, chosen = lax.top_k(score, requests)
        owners = (chosen // CAP)[jax.random.permutation(jax.random.fold_in(shard_key, 3), requests)]
        local_ids = jax.random.randint(jax.random.fold_in(shard_key, 4), (requests,), 0, QB_DEV)
        far_part = (owners * QB_DEV + local_ids).reshape(QB_DEV, NSEL - 1)
        own_part = shard * QB_DEV + jnp.arange(QB_DEV)
        return jnp.concatenate([own_part[:, None], far_part], axis=1)
    return jax.vmap(one_shard)(jnp.arange(SHARDS)).reshape(NQB, NSEL).astype(jnp.int32)


def levels(stream_key, dims, pieces, least, top_value):
    def one(axis_at, blocks):
        draws = jax.random.uniform(jax.random.fold_in(jax.random.fold_in(stream_key, 6), axis_at), (blocks,), jnp.float32, least / len(pieces), top_value / len(pieces))
        return jnp.repeat(jnp.exp(draws), dims[axis_at] // blocks).reshape((-1,) + (1,) * (len(dims) - axis_at - 1))

    level = one(*pieces[0])
    for cut in pieces[1:]:
        level = level * one(*cut)
    return level


def normal_values(own_key, shape, scale, limit, pieces=(), held_as=jnp.bfloat16):
    values = jax.random.normal(own_key, shape, jnp.float32) * scale
    if len(pieces) > 0:
        values = levels(own_key, shape, pieces, -0.22, 0.18) * values
    return jnp.clip(values, min=-limit, max=limit).astype(held_as)


def setup_inputs(seed: int = 0) -> dict:
    keys = jax.random.split(jax.random.key(seed), 10)
    return {
        "queries": draw_queries(jax.random.fold_in(keys[9], 71), 0),
        "key_rows": draw_key_rows(jax.random.fold_in(keys[9], 71), 0),
        "value_rows": normal_values(keys[2], (TOKEN_COUNT, D), 1.0, 6.0, ((0, 32), (1, 8))),
        "log_decay": draw_log_decay(jax.random.fold_in(keys[9], 71), 0),
        "write_rate": draw_write_rate(jax.random.fold_in(keys[9], 71), 0),
        "block_list": draw_block_list(jax.random.fold_in(keys[9], 71), 0),
        "attn_gain": jnp.clip(1.0 + 0.18 * jax.random.normal(keys[6], (D,), jnp.float32), 0.1, 1.9),
        "delta_gain": jnp.clip(1.0 + 0.18 * jax.random.normal(keys[7], (D,), jnp.float32), 0.1, 1.9),
        "out_weight": normal_values(keys[8], (D, D), D ** -0.5, 0.09375, ((0, 8),)),
    }


FULL_PRECISION = lax.Precision.HIGHEST

def unit_rows(values):
    return values * lax.rsqrt(lax.optimization_barrier(jnp.sum(values * values, axis=-1, keepdims=True)) + 1e-06)

def rms_scale(values):
    return values * lax.rsqrt(lax.optimization_barrier(jnp.mean(values * values, axis=-1, keepdims=True)) + 1e-06)

def block_terms(query_blk, key_blk, value_blk, decay_blk, rate_blk):
    length = decay_blk.shape[1]
    value_width = value_blk.shape[-1]
    key_width = key_blk.shape[-1]
    cumulative = jnp.cumsum(decay_blk, axis=1)
    row_number = lax.broadcasted_iota(jnp.int32, (length, length), 0)
    col_number = lax.broadcasted_iota(jnp.int32, (length, length), 1)
    inclusive = col_number <= row_number
    strict = col_number < row_number
    spread = cumulative[:, :, None] - cumulative[:, None, :]
    ratios = jnp.where(inclusive, jnp.exp(jnp.where(inclusive, spread, 0.0)), 0.0)
    key_key = jnp.einsum('htd,hsd->hts', key_blk, key_blk, precision=FULL_PRECISION)
    lower_part = jnp.where(strict, rate_blk[:, :, None] * ratios * key_key, 0.0)
    system = jnp.eye(length, dtype=jnp.float32) + lower_part
    growth = jnp.exp(cumulative)
    stacked = jnp.concatenate([rate_blk[:, :, None] * value_blk, (rate_blk * growth)[:, :, None] * key_blk], axis=-1)
    solved = jax.scipy.linalg.solve_triangular(system, stacked, lower=True, unit_diagonal=True)
    update = solved[..., :value_width]
    write_keys = solved[..., value_width:]
    attend = ratios * jnp.einsum('htd,hsd->hts', query_blk, key_blk, precision=FULL_PRECISION)
    local_out = jnp.einsum('hts,hse->hte', attend, update, precision=FULL_PRECISION)
    emit_rows = growth[:, :, None] * query_blk - jnp.einsum('hts,hsd->htd', attend, write_keys, precision=FULL_PRECISION)
    tail_decay = jnp.exp(cumulative[:, -1:] - cumulative)
    tailed = tail_decay[:, :, None] * key_blk
    transit = jnp.exp(cumulative[:, -1])[:, None, None] * jnp.eye(key_width, dtype=jnp.float32) - jnp.einsum('hcd,hce->hde', tailed, write_keys, precision=FULL_PRECISION)
    inject = jnp.einsum('hcd,hce->hde', tailed, update, precision=FULL_PRECISION)
    return (local_out, emit_rows, transit, inject)

def delta_branch(queries, key_rows, value_rows, log_decay, write_rate):
    block_shape = (NQB, BLK, HEAD_COUNT, HDIM)

    def advance(state_now, inputs):
        query_blk, key_blk, value_blk, decay_blk, rate_blk = inputs
        query_part = unit_rows(jnp.transpose(query_blk.astype(jnp.float32), (1, 0, 2)))
        key_part = unit_rows(jnp.transpose(key_blk.astype(jnp.float32), (1, 0, 2)))
        value_part = jnp.transpose(value_blk.astype(jnp.float32), (1, 0, 2))
        local_out, emit_rows, transit, inject = block_terms(query_part, key_part, value_part, jnp.transpose(decay_blk), jnp.transpose(rate_blk))
        result = local_out + jnp.einsum('htd,hde->hte', emit_rows, state_now, precision=FULL_PRECISION)
        state_next = jnp.einsum('hde,hef->hdf', transit, state_now, precision=FULL_PRECISION) + inject
        return (state_next, jnp.transpose(result, (1, 0, 2)))
    start_state = jnp.zeros((HEAD_COUNT, HDIM, HDIM), jnp.float32)
    _, outputs = lax.scan(advance, start_state, (queries.reshape(block_shape), key_rows.reshape(block_shape), value_rows.reshape(block_shape), log_decay.reshape(NQB, BLK, HEAD_COUNT), write_rate.reshape(NQB, BLK, HEAD_COUNT)))
    return outputs.reshape(TOKEN_COUNT, HEAD_COUNT, HDIM)

def attention_branch(queries, key_rows, value_rows, block_list):
    key_blocks = key_rows.reshape(NQB, BLK, HEAD_COUNT, HDIM)
    value_blocks = value_rows.reshape(NQB, BLK, HEAD_COUNT, HDIM)
    score_scale = HDIM ** (-0.5)

    def one_block(inputs):
        query_blk, listed = inputs
        keys_sel = key_blocks[listed].reshape(NSEL * BLK, HEAD_COUNT, HDIM).astype(jnp.float32)
        values_sel = value_blocks[listed].reshape(NSEL * BLK, HEAD_COUNT, HDIM).astype(jnp.float32)
        scores = jnp.einsum('ihd,jhd->hij', query_blk.astype(jnp.float32), keys_sel) * score_scale
        row_top = lax.optimization_barrier(jnp.max(scores, axis=-1, keepdims=True))
        shifted = jnp.exp(scores - row_top)
        weights = (shifted / lax.optimization_barrier(jnp.sum(shifted, axis=-1, keepdims=True))).astype(jnp.bfloat16)
        return jnp.einsum('hij,jhd->ihd', weights.astype(jnp.float32), values_sel)
    outputs = lax.map(one_block, (queries.reshape(NQB, BLK, HEAD_COUNT, HDIM), block_list))
    return outputs.reshape(TOKEN_COUNT, HEAD_COUNT, HDIM)

def reference(queries, key_rows, value_rows, log_decay, write_rate, block_list, attn_gain, delta_gain, out_weight):
    delta_out = delta_branch(queries, key_rows, value_rows, log_decay, write_rate)
    attn_out = attention_branch(queries, key_rows, value_rows, block_list)
    mixed_heads = rms_scale(attn_out) * attn_gain.reshape(HEAD_COUNT, HDIM) + rms_scale(delta_out) * delta_gain.reshape(HEAD_COUNT, HDIM)
    mixed_heads = mixed_heads.astype(jnp.bfloat16).reshape(TOKEN_COUNT, D)
    group_width = D // GROUPS
    total = jnp.zeros((TOKEN_COUNT, D), jnp.float32)
    for group in range(GROUPS):
        columns = mixed_heads[:, group * group_width:(group + 1) * group_width].astype(jnp.float32)
        rows_part = out_weight[group * group_width:(group + 1) * group_width].astype(jnp.float32)
        partial_value = jnp.dot(columns, rows_part, precision=FULL_PRECISION).astype(jnp.bfloat16)
        partial_value = lax.optimization_barrier(partial_value)
        total = total + partial_value.astype(jnp.float32)
    return total.astype(jnp.bfloat16)
```

```python
import functools

import jax
import jax.numpy as jnp
from jax import lax
from jax.experimental import pallas as pl
from jax.experimental.pallas import tpu as pltpu
from jax.sharding import Mesh
from jax.sharding import PartitionSpec as P

F32 = jnp.float32
BF16 = jnp.bfloat16
BLK = 64
NEG = -1e30


def ring(count, step):
    return [(source, (source + step) % count) for source in range(count)]


def mm(a, b, dims=((1,), (0,))):
    return lax.dot_general(
        a.astype(BF16), b.astype(BF16), (dims, ((), ())), preferred_element_type=F32
    )


def mm_hl(a, b):
    high = b.astype(BF16)
    low = (b - high.astype(F32)).astype(BF16)
    return mm(a, high) + mm(a, low)


def delta_kernel(q_ref, k_ref, v_ref, col_ref, row_ref, local_ref, emit_ref, ti_ref, *, heads):
    head = pl.program_id(0)
    q, k, v = q_ref[...], k_ref[...], v_ref[...]
    tokens = k.shape[0]
    qf, kf, vf = q.astype(F32), k.astype(F32), v.astype(F32)
    nk = lax.rsqrt(jnp.sum(kf * kf, axis=1, keepdims=True) + 1e-06)
    nq = lax.rsqrt(jnp.sum(qf * qf, axis=1, keepdims=True) + 1e-06)
    cols = col_ref[...]
    lane = lax.broadcasted_iota(jnp.int32, cols.shape, 1)
    d_col = jnp.sum(jnp.where(lane == head, cols, 0.0), axis=1, keepdims=True)
    b_col = jnp.sum(jnp.where(lane == head + heads, cols, 0.0), axis=1, keepdims=True)
    d_row = row_ref[pl.ds(head, 1), :]
    b_row = row_ref[pl.ds(head + heads, 1), :]
    ri = lax.broadcasted_iota(jnp.int32, (tokens, tokens), 0)
    ci = lax.broadcasted_iota(jnp.int32, (tokens, tokens), 1)
    incl = ci <= ri
    c_col = jnp.sum(jnp.where(incl, d_row, 0.0), axis=1, keepdims=True)
    c_row = jnp.sum(jnp.where(ri <= ci, d_col, 0.0), axis=0, keepdims=True)
    nk_row = jnp.sum(jnp.where(ri == ci, nk, 0.0), axis=0, keepdims=True)
    decay = jnp.where(incl, jnp.exp(jnp.where(incl, c_col - c_row, 0.0)) * nk_row, 0.0)
    kk = mm(k, k, ((1,), (1,)))
    qk = mm(q, k, ((1,), (1,)))
    low = jnp.where(ci < ri, decay * kk * (b_col * nk), 0.0)
    attend = decay * qk * nq
    differ = ri ^ ci
    off = jnp.where(differ < 2, -low, 0.0)
    size = 2
    while size < tokens:
        part = jnp.where((differ >= size) & (differ < 2 * size), low, 0.0)
        left = part + mm(off, part)
        off = off - (left + mm(left, off))
        size *= 2
    g_col, g_row = jnp.exp(c_col), jnp.exp(c_row)
    update = b_col * vf + mm(off * b_row, v)
    keyed = (b_col * g_col * nk) * kf + mm(off * (b_row * g_row * nk_row), k)
    both = jnp.concatenate([update, keyed], axis=1)
    seen = mm(attend, both)
    width = v.shape[1]
    local_ref[0] = seen[:, :width]
    emit_ref[0] = ((g_col * nq) * qf - seen[:, width:]).astype(BF16)
    c_end = c_col[tokens - 1 : tokens, :]
    tail = jnp.exp(c_end - c_col) * nk
    ends = mm(k, tail * both, ((0,), (0,)))
    er = lax.broadcasted_iota(jnp.int32, (width, width), 0)
    ec = lax.broadcasted_iota(jnp.int32, (width, width), 1)
    transit = jnp.where(er == ec, jnp.exp(c_end), 0.0) - ends[:, width:]
    ti_ref[0] = jnp.concatenate([transit, ends[:, :width]], axis=1).astype(BF16)


def delta_local(queries, key_rows, value_rows, cols, rows, heads):
    tokens, packed = queries.shape
    width = packed // heads
    token_spec = pl.BlockSpec((tokens, width), lambda h: (0, h))
    return pl.pallas_call(
        functools.partial(delta_kernel, heads=heads),
        grid=(heads,),
        in_specs=[
            token_spec,
            token_spec,
            token_spec,
            pl.BlockSpec(cols.shape, lambda h: (0, 0)),
            pl.BlockSpec(rows.shape, lambda h: (0, 0)),
        ],
        out_specs=[
            pl.BlockSpec((1, tokens, width), lambda h: (h, 0, 0)),
            pl.BlockSpec((1, tokens, width), lambda h: (h, 0, 0)),
            pl.BlockSpec((1, width, 2 * width), lambda h: (h, 0, 0)),
        ],
        out_shape=[
            jax.ShapeDtypeStruct((heads, tokens, width), F32),
            jax.ShapeDtypeStruct((heads, tokens, width), BF16),
            jax.ShapeDtypeStruct((heads, width, 2 * width), BF16),
        ],
        name="delta_local",
        cost_estimate=pl.CostEstimate(flops=4_000_000_000, bytes_accessed=3_000_000, transcendentals=0),
    )(queries, key_rows, value_rows, cols, rows)


def row_kernel(ti_ref, out_ref):
    members, width, _ = ti_ref.shape
    acc = ti_ref[0].astype(F32)
    for member in range(1, members):
        step = ti_ref[member]
        acc = mm_hl(step[:, :width], acc)
        acc = acc + jnp.concatenate(
            [jnp.zeros((width, width), F32), step[:, width:].astype(F32)], axis=1
        )
    out_ref[...] = acc.astype(BF16)


def row_compose(ti_row):
    _, width, double = ti_row.shape
    return pl.pallas_call(
        row_kernel,
        out_shape=jax.ShapeDtypeStruct((width, double), BF16),
        name="row_compose",
        cost_estimate=pl.CostEstimate(flops=100_000_000, bytes_accessed=400_000, transcendentals=0),
    )(ti_row)


def states_kernel(z_ref, group_ref, ti_ref, out_ref):
    members, width, _ = ti_ref.shape

    def advance(state, step):
        return mm_hl(step[:, :width], state) + step[:, width:].astype(F32)

    state = lax.fori_loop(
        0,
        z_ref[0],
        lambda i, state: advance(state, group_ref[i]),
        jnp.zeros((width, width), F32),
    )
    for member in range(members):
        out_ref[member] = state.astype(BF16)
        if member + 1 < members:
            state = advance(state, ti_ref[member])


def entry_states(z_pos, groups, ti_row):
    members, width, _ = ti_row.shape
    return pl.pallas_call(
        states_kernel,
        in_specs=[
            pl.BlockSpec(memory_space=pltpu.SMEM),
            pl.BlockSpec(memory_space=pltpu.VMEM),
            pl.BlockSpec(memory_space=pltpu.VMEM),
        ],
        out_shape=jax.ShapeDtypeStruct((members, width, width), BF16),
        name="entry_states",
        cost_estimate=pl.CostEstimate(flops=100_000_000, bytes_accessed=800_000, transcendentals=0),
    )(z_pos, groups, ti_row)


def attend_kernel(pos_ref, list_ref, *refs, rows, cols, head_dim, lanes):
    q_hbm, kv_hbm = refs[:rows], refs[rows : rows + cols]
    out_ref = refs[rows + cols]
    q_ref, kv_ref, m_ref, l_ref, acc_ref, lse_ref, sems = refs[rows + cols + 1 :]
    my_z, my_y = pos_ref[0], pos_ref[1]
    copies = [pltpu.make_async_copy(src, q_ref.at[i], sems.at[i]) for i, src in enumerate(q_hbm)]
    copies += [
        pltpu.make_async_copy(src, kv_ref.at[i], sems.at[rows + i]) for i, src in enumerate(kv_hbm)
    ]
    for copy in copies:
        copy.start()
    for copy in copies:
        copy.wait()
    tokens = q_ref.shape[1]
    blocks = tokens // BLK
    heads = q_ref.shape[2] // head_dim
    listed = list_ref.shape[1]
    scale = head_dim ** (-0.5)
    lane = lax.broadcasted_iota(jnp.int32, (BLK, lanes), 1)

    def one_block(index, _):
        away, blk = index // blocks, index % blocks
        token = pl.multiple_of(blk * BLK, BLK)
        m_ref[...] = jnp.full(m_ref.shape, NEG, F32)
        l_ref[...] = jnp.zeros(l_ref.shape, F32)
        acc_ref[...] = jnp.zeros(acc_ref.shape, F32)
        for entry in range(listed):
            name = list_ref[index, entry]
            shard = name // blocks
            place = pl.multiple_of((name % blocks) * BLK, BLK)
            slot = (my_z - shard // rows + cols) % cols

            @pl.when(shard % rows == my_y)
            def _():
                for h in range(heads):
                    q = q_ref[away, pl.ds(token, BLK), h * head_dim : (h + 1) * head_dim]
                    k = kv_ref[slot, pl.ds(place, BLK), h * head_dim : (h + 1) * head_dim]
                    v = kv_ref[
                        slot, pl.ds(place, BLK), (heads + h) * head_dim : (heads + h + 1) * head_dim
                    ]
                    s = mm(q, k, ((1,), (1,))) * scale
                    m_old = m_ref[h]
                    m_new = jnp.maximum(m_old, jnp.max(s, axis=1, keepdims=True))
                    p = jnp.exp(s - m_new[:, :1])
                    fade = jnp.exp(m_old - m_new)
                    l_ref[h] = fade * l_ref[h] + jnp.sum(p, axis=1, keepdims=True)
                    acc_ref[h] = fade * acc_ref[h] + mm(p, v)
                    m_ref[h] = m_new

        target = (my_y - away + rows) % rows
        parts = jnp.zeros((BLK, lanes), F32)
        for h in range(heads):
            total = l_ref[h]
            some = total > 0.0
            out_ref[target, pl.ds(token, BLK), h * head_dim : (h + 1) * head_dim] = (
                acc_ref[h] / jnp.where(some, total, 1.0)
            ).astype(BF16)
            lse = jnp.where(some, m_ref[h] + jnp.log(jnp.where(some, total, 1.0)), NEG)
            for piece in range(3):
                top = lse.astype(BF16).astype(F32)
                parts = jnp.where(lane == 3 * h + piece, top, parts)
                lse = lse - top
        lse_ref[target, pl.ds(token, BLK), :] = parts
        return 0

    lax.fori_loop(0, rows * blocks, one_block, 0)
    for target in range(rows):
        turned = jnp.transpose(lse_ref[target])[:16, :]
        out_ref[target, tokens:, :tokens] = turned.astype(BF16)


def attend_part(pos, lists, q_arrays, kv_arrays, heads, head_dim):
    rows, cols = len(q_arrays), len(kv_arrays)
    tokens = q_arrays[0].shape[0]
    packed = heads * head_dim
    any_spec = pl.BlockSpec(memory_space=pl.ANY)
    smem = pl.BlockSpec(memory_space=pltpu.SMEM)
    return pl.pallas_call(
        functools.partial(attend_kernel, rows=rows, cols=cols, head_dim=head_dim, lanes=128),
        in_specs=[smem, smem] + [any_spec] * (rows + cols),
        out_specs=pl.BlockSpec(memory_space=pltpu.VMEM),
        out_shape=jax.ShapeDtypeStruct((rows, tokens + 16, packed), BF16),
        scratch_shapes=[
            pltpu.VMEM((rows, tokens, packed), BF16),
            pltpu.VMEM((cols, tokens, 2 * packed), BF16),
            pltpu.VMEM((heads, BLK, 128), F32),
            pltpu.VMEM((heads, BLK, 128), F32),
            pltpu.VMEM((heads, BLK, head_dim), F32),
            pltpu.VMEM((rows, tokens, 128), F32),
            pltpu.SemaphoreType.DMA((rows + cols,)),
        ],
        name="attend_part",
        cost_estimate=pl.CostEstimate(flops=3_000_000_000, bytes_accessed=3_000_000, transcendentals=0),
    )(pos, lists, *q_arrays, *kv_arrays)


def mix_kernel(
    core_ref, parts_ref, local_ref, emit_ref, state_ref, again_ref, dgain_ref, w_ref,
    keep_ref, send_ref, mixed_ref, order_ref,
):
    sources, padded, packed = parts_ref.shape
    heads, tokens, width = local_ref.shape
    half = tokens // 2
    rows = keep_ref.shape[1]

    @pl.when(pl.program_id(0) == 0)
    def _():
        lses = []
        for s in range(sources):
            turned = jnp.transpose(parts_ref[s, tokens:, :tokens].astype(F32))
            lane = lax.broadcasted_iota(jnp.int32, turned.shape, 1)
            lses.append(
                [
                    jnp.sum(
                        jnp.where((lane >= 3 * h) & (lane < 3 * h + 3), turned, 0.0),
                        axis=1,
                        keepdims=True,
                    )
                    for h in range(heads)
                ]
            )
        for h in range(heads):
            span = slice(h * width, (h + 1) * width)
            top = functools.reduce(jnp.maximum, [lses[s][h] for s in range(sources)])
            shares = [jnp.exp(lses[s][h] - top) for s in range(sources)]
            total = functools.reduce(jnp.add, shares)
            attn = functools.reduce(
                jnp.add,
                [(shares[s] / total) * parts_ref[s, :tokens, span].astype(F32) for s in range(sources)],
            )
            delta = local_ref[h] + mm(emit_ref[h], state_ref[h])
            mixed = attn * lax.rsqrt(
                jnp.mean(attn * attn, axis=1, keepdims=True) + 1e-06
            ) * again_ref[:, span] + delta * lax.rsqrt(
                jnp.mean(delta * delta, axis=1, keepdims=True) + 1e-06
            ) * dgain_ref[:, span]
            mixed_ref[:, span] = mixed
        core = core_ref[0]
        for x in range(keep_ref.shape[0]):
            near = pl.multiple_of((2 * x + core) * rows, rows)
            far = pl.multiple_of((2 * x + 1 - core) * rows, rows)
            order_ref[x * rows : (x + 1) * rows, :] = mixed_ref[pl.ds(near, rows), :].astype(BF16)
            order_ref[half + x * rows : half + (x + 1) * rows, :] = mixed_ref[
                pl.ds(far, rows), :
            ].astype(BF16)

    out = mm(order_ref[...], w_ref[...]).astype(BF16)
    keep_ref[...] = out[:half].reshape(keep_ref.shape)
    send_ref[...] = out[half:].reshape(send_ref.shape)


def mix_project(core, parts, local_out, emit, states, attn_gain, delta_gain, out_weight, xs):
    heads, tokens, width = local_out.shape
    packed, model = out_weight.shape
    rows = tokens // (2 * xs)
    tile = min(1024, model)

    def whole(array):
        return pl.BlockSpec(array.shape, lambda n: (0,) * array.ndim)

    out_spec = pl.BlockSpec((xs, rows, tile), lambda n: (0, 0, n))
    out_shape = jax.ShapeDtypeStruct((xs, rows, model), BF16)
    return pl.pallas_call(
        mix_kernel,
        grid=(model // tile,),
        in_specs=[pl.BlockSpec(memory_space=pltpu.SMEM)]
        + [whole(array) for array in (parts, local_out, emit, states, attn_gain, delta_gain)]
        + [pl.BlockSpec((packed, tile), lambda n: (0, n))],
        out_specs=[out_spec, out_spec],
        out_shape=[out_shape, out_shape],
        scratch_shapes=[pltpu.VMEM((tokens, packed), F32), pltpu.VMEM((tokens, packed), BF16)],
        name="mix_project",
        cost_estimate=pl.CostEstimate(flops=1_200_000_000, bytes_accessed=8_000_000, transcendentals=0),
    )(core, parts, local_out, emit, states, attn_gain, delta_gain, out_weight)


def body(
    queries, key_rows, value_rows, log_decay, write_rate, block_list, attn_gain, delta_gain, out_weight
):
    tokens, packed = queries.shape
    heads = log_decay.shape[1]
    head_dim = packed // heads
    zs, ys, xs = lax.axis_size("z"), lax.axis_size("y"), lax.axis_size("x")
    z_pos, y_pos, core = lax.axis_index("z"), lax.axis_index("y"), lax.axis_index("core")

    cols = jnp.concatenate([log_decay, write_rate], axis=1)
    kv = jnp.concatenate([key_rows, value_rows], axis=1)

    forward, backward = [kv], [kv]
    for distance in range(1, zs // 2 + 1):
        forward.append(lax.ppermute(forward[-1], "z", ring(zs, 1)))
        if distance < zs - distance:
            backward.append(lax.ppermute(backward[-1], "z", ring(zs, -1)))
    kv_arrays = [
        forward[distance] if distance <= zs // 2 else backward[zs - distance] for distance in range(zs)
    ]

    q_arrays, lists = [queries], [block_list]
    for distance in range(1, ys):
        q_arrays.append(lax.ppermute(queries, "y", ring(ys, distance)))
        lists.append(lax.ppermute(block_list, "y", ring(ys, distance)))
    lists = jnp.concatenate(lists, axis=0)

    local_out, emit, ti = delta_local(
        queries, key_rows, value_rows, cols, jnp.transpose(cols), heads
    )
    ti_row = lax.all_to_all(ti, "y", split_axis=0, concat_axis=0, tiled=True)
    group = row_compose(ti_row)
    groups = lax.all_to_all(
        jnp.broadcast_to(group[None], (zs,) + group.shape), "z", split_axis=0, concat_axis=0, tiled=True
    )
    states = entry_states(z_pos[None].astype(jnp.int32), groups, ti_row)
    states = lax.all_to_all(states, "y", split_axis=0, concat_axis=0, tiled=True)

    pos = jnp.stack([z_pos, y_pos]).astype(jnp.int32)
    parts = attend_part(pos, lists, q_arrays, kv_arrays, heads, head_dim)
    parts = lax.all_to_all(parts, "y", split_axis=0, concat_axis=0, tiled=True)

    keep, send = mix_project(
        core[None].astype(jnp.int32),
        parts,
        local_out,
        emit,
        states,
        attn_gain[None],
        delta_gain[None],
        out_weight,
        xs,
    )
    got = lax.ppermute(send, "core", [(0, 1), (1, 0)])
    pair = (keep.astype(F32) + got.astype(F32)).astype(BF16)
    spread = lax.all_to_all(pair, "x", split_axis=0, concat_axis=0, tiled=True)
    return jnp.sum(spread.astype(F32), axis=0).astype(BF16)


def solution(mesh):
    ys = 4
    cores = 2
    grid = mesh.devices.reshape(
        mesh.shape["heads"] // cores, cores, mesh.shape["ctx"] // ys, ys
    )
    fine = Mesh(grid, ("x", "core", "z", "y"))
    heads, ctx = ("x", "core"), ("z", "y")
    in_specs = (
        P(ctx, heads),
        P(ctx, heads),
        P(ctx, heads),
        P(ctx, heads),
        P(ctx, heads),
        P(ctx, None),
        P(heads),
        P(heads),
        P(heads, None),
    )
    out_specs = P(ctx + heads, None)
    return jax.shard_map(body, mesh=fine, in_specs=in_specs, out_specs=out_specs, check_vma=False)
```

```python
import functools

import jax
import jax.numpy as jnp
from jax import lax
from jax.experimental import pallas as pl
from jax.experimental.pallas import tpu as pltpu
from jax.sharding import Mesh
from jax.sharding import PartitionSpec as P


F32 = jnp.float32
BF16 = jnp.bfloat16
BLK = 64
VMEM = 16 * 1024 * 1024
NEG = -1e30


def ring(count, step):
    return [(source, (source + step) % count) for source in range(count)]


def mm(a, b, dims=((1,), (0,))):
    return lax.dot_general(
        a.astype(BF16), b.astype(BF16), (dims, ((), ())), preferred_element_type=F32
    )


def mm_hl(a, b):
    high = b.astype(BF16)
    low = (b - high.astype(F32)).astype(BF16)
    return mm(a, high) + mm(a, low)


def delta_kernel(
    q_ref, k_ref, v_ref, decay_ref, rate_ref, list_ref, local_ref, emit_ref, ti_ref
):
    head = pl.program_id(0)
    q, k, v = q_ref[...], k_ref[...], v_ref[...]
    tokens = k.shape[0]
    qf, kf, vf = q.astype(F32), k.astype(F32), v.astype(F32)
    nk = lax.rsqrt(jnp.sum(kf * kf, axis=1, keepdims=True) + 1e-06)
    nq = lax.rsqrt(jnp.sum(qf * qf, axis=1, keepdims=True) + 1e-06)
    d_row = decay_ref[pl.ds(head, 1), :]
    b_row = rate_ref[pl.ds(head, 1), :]
    ri = lax.broadcasted_iota(jnp.int32, (tokens, tokens), 0)
    ci = lax.broadcasted_iota(jnp.int32, (tokens, tokens), 1)
    incl = ci <= ri
    d_col = jnp.sum(jnp.where(ri == ci, d_row, 0.0), axis=1, keepdims=True)
    b_col = jnp.sum(jnp.where(ri == ci, b_row, 0.0), axis=1, keepdims=True)
    c_col = jnp.sum(jnp.where(incl, d_row, 0.0), axis=1, keepdims=True)
    c_row = jnp.sum(jnp.where(ri <= ci, d_col, 0.0), axis=0, keepdims=True)
    nk_row = jnp.sum(jnp.where(ri == ci, nk, 0.0), axis=0, keepdims=True)
    decay = jnp.where(incl, jnp.exp(jnp.where(incl, c_col - c_row, 0.0)) * nk_row, 0.0)
    kk = mm(k, k, ((1,), (1,)))
    qk = mm(q, k, ((1,), (1,)))
    low = jnp.where(ci < ri, decay * kk * (b_col * nk), 0.0)
    attend = decay * qk * nq
    differ = ri ^ ci
    off = jnp.where(differ < 2, -low, 0.0)
    size = 2
    while size < tokens:
        part = jnp.where((differ >= size) & (differ < 2 * size), low, 0.0)
        left = part + mm(off, part)
        off = off - (left + mm(left, off))
        size *= 2
    g_col, g_row = jnp.exp(c_col), jnp.exp(c_row)
    update = b_col * vf + mm(off * b_row, v)
    keyed = (b_col * g_col * nk) * kf + mm(off * (b_row * g_row * nk_row), k)
    both = jnp.concatenate([update, keyed], axis=1)
    seen = mm(attend, both)
    width = v.shape[1]
    local_ref[0] = seen[:, :width]
    emit_ref[0] = ((g_col * nq) * qf - seen[:, width:]).astype(BF16)
    c_end = c_col[tokens - 1 : tokens, :]
    tail = jnp.exp(c_end - c_col) * nk
    ends = mm(k, tail * both, ((0,), (0,)))
    er = lax.broadcasted_iota(jnp.int32, (width, width), 0)
    ec = lax.broadcasted_iota(jnp.int32, (width, width), 1)
    transit = jnp.where(er == ec, jnp.exp(c_end), 0.0) - ends[:, width:]
    ti_ref[0, :width] = jnp.concatenate([transit, ends[:, :width]], axis=1).astype(BF16)
    note = ti_ref.shape[1] - width
    nr = lax.broadcasted_iota(jnp.int32, (note, 2 * width), 0)
    nc = lax.broadcasted_iota(jnp.int32, (note, 2 * width), 1)
    names = jnp.zeros((note, 2 * width), jnp.int32)
    for entry in range(list_ref.shape[0]):
        for blk in range(list_ref.shape[1]):
            names = jnp.where((nr == blk) & (nc == entry), list_ref[entry, blk], names)
    ti_ref[0, width:] = names.astype(F32).astype(BF16)


def delta_local(queries, key_rows, value_rows, decay, rate, names):
    tokens, packed = queries.shape
    heads = decay.shape[0]
    width = packed // heads
    token_spec = pl.BlockSpec((tokens, width), lambda h: (0, h))
    return pl.pallas_call(
        delta_kernel,
        grid=(heads,),
        in_specs=[
            token_spec,
            token_spec,
            token_spec,
            pl.BlockSpec(decay.shape, lambda h: (0, 0)),
            pl.BlockSpec(rate.shape, lambda h: (0, 0)),
            pl.BlockSpec(memory_space=pltpu.SMEM),
        ],
        out_specs=[
            pl.BlockSpec((1, tokens, width), lambda h: (h, 0, 0)),
            pl.BlockSpec((1, tokens, width), lambda h: (h, 0, 0)),
            pl.BlockSpec((1, width + 16, 2 * width), lambda h: (h, 0, 0)),
        ],
        out_shape=[
            jax.ShapeDtypeStruct((heads, tokens, width), F32),
            jax.ShapeDtypeStruct((heads, tokens, width), BF16),
            jax.ShapeDtypeStruct((heads, width + 16, 2 * width), BF16),
        ],
        name="delta_local",
        cost_estimate=pl.CostEstimate(flops=4_000_000_000, bytes_accessed=3_000_000, transcendentals=0),
    )(queries, key_rows, value_rows, decay, rate, names)


def row_kernel(ti_ref, out_ref):
    members = ti_ref.shape[0]
    width = ti_ref.shape[2] // 2
    acc = ti_ref[0, :width].astype(F32)
    for member in range(1, members):
        step = ti_ref[member, :width]
        acc = mm_hl(step[:, :width], acc)
        acc = acc + jnp.concatenate(
            [jnp.zeros((width, width), F32), step[:, width:].astype(F32)], axis=1
        )
    out = acc.astype(BF16)
    for copy in range(out_ref.shape[0]):
        out_ref[copy] = out


def row_compose(ti_row, copies):
    double = ti_row.shape[2]
    width = double // 2
    return pl.pallas_call(
        row_kernel,
        out_shape=jax.ShapeDtypeStruct((copies, width, double), BF16),
        name="row_compose",
        compiler_params=pltpu.CompilerParams(vmem_limit_bytes=VMEM),
        cost_estimate=pl.CostEstimate(flops=100_000_000, bytes_accessed=400_000, transcendentals=0),
    )(ti_row)


def states_kernel(z_ref, group_ref, ti_ref, out_ref):
    members = ti_ref.shape[0]
    width = ti_ref.shape[2] // 2

    def advance(state, step):
        return mm_hl(step[:, :width], state) + step[:, width:].astype(F32)

    state = lax.fori_loop(
        0,
        z_ref[0],
        lambda i, state: advance(state, group_ref[i]),
        jnp.zeros((width, width), F32),
    )
    for member in range(members):
        out_ref[member] = state.astype(BF16)
        if member + 1 < members:
            state = advance(state, ti_ref[member, :width])


def entry_states(z_pos, groups, ti_row):
    members = ti_row.shape[0]
    width = ti_row.shape[2] // 2
    return pl.pallas_call(
        states_kernel,
        in_specs=[
            pl.BlockSpec(memory_space=pltpu.SMEM),
            pl.BlockSpec(memory_space=pltpu.VMEM),
            pl.BlockSpec(memory_space=pltpu.VMEM),
        ],
        out_shape=jax.ShapeDtypeStruct((members, width, width), BF16),
        name="entry_states",
        compiler_params=pltpu.CompilerParams(vmem_limit_bytes=VMEM),
        cost_estimate=pl.CostEstimate(flops=100_000_000, bytes_accessed=800_000, transcendentals=0),
    )(z_pos, groups, ti_row)


def attend_kernel(pos_ref, list_ref, *refs, rows, cols, slots, head_dim):
    q_hbm, kv_hbm = refs[:rows], refs[rows : rows + len(slots)]
    outs = refs[rows + len(slots) : 2 * rows + len(slots)]
    q_ref, kv_ref, lse_ref, sems = refs[2 * rows + len(slots) :]
    tokens, packed = q_hbm[0].shape
    heads = packed // head_dim
    pair = 2 * head_dim
    stages = []
    for stage in range(heads // 2):
        span = pl.ds(stage * pair, pair)
        copies = []
        for i, src in enumerate(q_hbm):
            dst = q_ref.at[stage, pl.ds(i * tokens, tokens)]
            copies.append(
                pltpu.make_async_copy(src.at[:, span], dst, sems.at[stage, len(copies)])
            )
        for start, src in zip(slots, kv_hbm):
            dst = kv_ref.at[stage, pl.ds(start, src.shape[0])]
            copies.append(
                pltpu.make_async_copy(src.at[:, span], dst, sems.at[stage, len(copies)])
            )
        stages.append(copies)
    for copies in stages:
        for copy in copies:
            copy.start()
    blocks = tokens // BLK
    listed = list_ref.shape[2]
    scale = head_dim ** (-0.5)
    lane = lax.broadcasted_iota(jnp.int32, (BLK, 128), 1)
    part = lax.broadcasted_iota(jnp.int32, (1, listed * BLK), 1) // BLK
    blank = jnp.zeros((BLK, head_dim), BF16)
    my_z, my_y = pos_ref[0], pos_ref[1]

    def attend(stage, away, blk, place):
        member = lax.rem(my_y - away + rows, rows)
        starts, held = [], jnp.zeros(part.shape, jnp.int32)
        for entry in range(listed):
            name = list_ref[member, blk, entry]
            shard = lax.div(name, blocks)
            line = lax.div(shard, rows)
            slot = lax.rem(my_z - line + cols, cols)
            starts.append(
                pl.multiple_of(slot * (2 * tokens) + (name - shard * blocks) * BLK, BLK)
            )
            here = (shard - line * rows == my_y).astype(jnp.int32)
            held = jnp.where(part == entry, here, held)
        row = pl.multiple_of(away * tokens + blk * BLK, BLK)
        q = q_ref[stage, pl.ds(row, BLK), :]
        q = jnp.concatenate(
            [
                jnp.concatenate([q[:, :head_dim], blank], axis=1),
                jnp.concatenate([blank, q[:, head_dim:]], axis=1),
            ],
            axis=0,
        )
        k = jnp.concatenate([kv_ref[stage, pl.ds(start, BLK), :] for start in starts], axis=0)
        v = jnp.concatenate(
            [kv_ref[stage, pl.ds(start + tokens, BLK), :] for start in starts], axis=0
        )
        s = jnp.where(held > 0, mm(q, k, ((1,), (1,))) * scale, NEG)
        top = jnp.max(s, axis=1, keepdims=True)
        p = jnp.exp(s - top)
        total = jnp.sum(p, axis=1, keepdims=True)
        o = mm(p, v) * (1.0 / total)
        out = outs[away]
        left = slice(stage * pair, stage * pair + head_dim)
        right = slice(stage * pair + head_dim, (stage + 1) * pair)
        out[place, left] = o[:BLK, :head_dim].astype(BF16)
        out[place, right] = o[BLK:, head_dim:].astype(BF16)
        lse = top + jnp.log(total)
        rest = lse_ref[pl.ds(row, BLK), :]
        lse_ref[pl.ds(row, BLK), :] = jnp.where(
            lane == 2 * stage, lse[:BLK], jnp.where(lane == 2 * stage + 1, lse[BLK:], rest)
        )

    for stage, copies in enumerate(stages):
        for copy in copies:
            copy.wait()

        def some_blocks(blk, _, stage=stage):
            for away in range(rows):
                attend(stage, away, blk, pl.ds(pl.multiple_of(blk * BLK, BLK), BLK))
            return 0

        lax.fori_loop(0, blocks, some_blocks, 0)
    for away in range(rows):
        rest = jnp.transpose(lse_ref[away * tokens : (away + 1) * tokens, :])[:8, :]
        pieces = []
        for _ in range(3):
            high = rest.astype(BF16).astype(F32)
            pieces.append(high)
            rest = rest - high
        outs[away][tokens:, :tokens] = jnp.concatenate(pieces[:2], axis=0).astype(BF16)
        outs[away][tokens:, tokens:] = jnp.concatenate(
            [pieces[2], jnp.zeros_like(rest)], axis=0
        ).astype(BF16)


def attend_part(pos, lists, q_arrays, kv_arrays, slots, heads, head_dim, cols):
    rows = len(q_arrays)
    tokens = q_arrays[0].shape[0]
    packed = heads * head_dim
    stages = heads // 2
    smem = pl.BlockSpec(memory_space=pltpu.SMEM)
    any_spec = pl.BlockSpec(memory_space=pl.ANY)
    return pl.pallas_call(
        functools.partial(
            attend_kernel, rows=rows, cols=cols, slots=tuple(slots), head_dim=head_dim
        ),
        in_specs=[smem, smem] + [any_spec] * (rows + len(kv_arrays)),
        out_specs=[pl.BlockSpec(memory_space=pltpu.VMEM)] * rows,
        out_shape=[jax.ShapeDtypeStruct((tokens + 16, packed), BF16)] * rows,
        scratch_shapes=[
            pltpu.VMEM((stages, rows * tokens, 2 * head_dim), BF16),
            pltpu.VMEM((stages, 2 * cols * tokens, 2 * head_dim), BF16),
            pltpu.VMEM((rows * tokens, 128), F32),
            pltpu.SemaphoreType.DMA((stages, rows + len(kv_arrays))),
        ],
        name="attend_part",
        compiler_params=pltpu.CompilerParams(vmem_limit_bytes=VMEM),
        cost_estimate=pl.CostEstimate(flops=3_000_000_000, bytes_accessed=6_000_000, transcendentals=0),
    )(pos, lists, *q_arrays, *kv_arrays)


def mix_kernel(
    core_ref, local_ref, emit_ref, state_ref, again_ref, dgain_ref, w_ref, *refs
):
    parts, (keep_ref, send_ref, order_ref, mixed_ref) = refs[:-4], refs[-4:]
    sources = len(parts)
    heads, tokens, width = local_ref.shape
    half = tokens // 2
    rows = keep_ref.shape[1]

    @pl.when(pl.program_id(0) == 0)
    def _():
        lses = []
        for s in range(sources):
            pieces = parts[s][tokens:, :].astype(F32)
            rows8 = pieces[:8, :tokens] + pieces[8:, :tokens] + pieces[:8, tokens:]
            turned = jnp.transpose(rows8)
            lane = lax.broadcasted_iota(jnp.int32, turned.shape, 1)
            lses.append(
                [
                    jnp.sum(jnp.where(lane == h, turned, 0.0), axis=1, keepdims=True)
                    for h in range(heads)
                ]
            )
        for h in range(heads):
            span = slice(h * width, (h + 1) * width)
            top = functools.reduce(jnp.maximum, [lses[s][h] for s in range(sources)])
            shares = [jnp.exp(lses[s][h] - top) for s in range(sources)]
            total = functools.reduce(jnp.add, shares)
            attn = functools.reduce(
                jnp.add,
                [(shares[s] / total) * parts[s][:tokens, span].astype(F32) for s in range(sources)],
            )
            delta = local_ref[h] + mm(emit_ref[h], state_ref[h])
            mixed = attn * lax.rsqrt(
                jnp.mean(attn * attn, axis=1, keepdims=True) + 1e-06
            ) * again_ref[:, span] + delta * lax.rsqrt(
                jnp.mean(delta * delta, axis=1, keepdims=True) + 1e-06
            ) * dgain_ref[:, span]
            mixed_ref[:, span] = mixed
        core = core_ref[0]
        for x in range(keep_ref.shape[0]):
            near = pl.multiple_of((2 * x + core) * rows, rows)
            far = pl.multiple_of((2 * x + 1 - core) * rows, rows)
            order_ref[x * rows : (x + 1) * rows, :] = mixed_ref[pl.ds(near, rows), :].astype(BF16)
            order_ref[half + x * rows : half + (x + 1) * rows, :] = mixed_ref[
                pl.ds(far, rows), :
            ].astype(BF16)

    project_kernel(order_ref, w_ref, keep_ref, send_ref)


def project_kernel(order_ref, w_ref, keep_ref, send_ref):
    half = order_ref.shape[0] // 2
    out = mm(order_ref[...], w_ref[...]).astype(BF16)
    keep_ref[...] = out[:half].reshape(keep_ref.shape)
    send_ref[...] = out[half:].reshape(send_ref.shape)


def tail_specs(tokens, packed, xs, first, count, tile):
    rows = tokens // (2 * xs)
    return (
        pl.BlockSpec((packed, tile), lambda n: (0, first + n)),
        pl.BlockSpec((xs, rows, tile), lambda n: (0, 0, n)),
        jax.ShapeDtypeStruct((xs, rows, count * tile), BF16),
    )


def mix_project(core, parts, local_out, emit, states, attn_gain, delta_gain, out_weight, xs, tile, count):
    _, tokens, _ = local_out.shape
    packed, _ = out_weight.shape

    def whole(array):
        return pl.BlockSpec(array.shape, lambda n: (0,) * array.ndim)

    w_spec, out_spec, out_shape = tail_specs(tokens, packed, xs, 0, count, tile)
    return pl.pallas_call(
        mix_kernel,
        grid=(count,),
        in_specs=[pl.BlockSpec(memory_space=pltpu.SMEM)]
        + [whole(array) for array in (local_out, emit, states, attn_gain, delta_gain)]
        + [w_spec]
        + [whole(array) for array in parts],
        out_specs=[out_spec, out_spec, pl.BlockSpec((tokens, packed), lambda n: (0, 0))],
        out_shape=[out_shape, out_shape, jax.ShapeDtypeStruct((tokens, packed), BF16)],
        scratch_shapes=[pltpu.VMEM((tokens, packed), F32)],
        name="mix_project",
        cost_estimate=pl.CostEstimate(flops=800_000_000, bytes_accessed=5_000_000, transcendentals=0),
    )(core, local_out, emit, states, attn_gain, delta_gain, out_weight, *parts)


def project(order, out_weight, xs, tile, first, count):
    tokens, packed = order.shape
    w_spec, out_spec, out_shape = tail_specs(tokens, packed, xs, first, count, tile)
    return pl.pallas_call(
        project_kernel,
        grid=(count,),
        in_specs=[pl.BlockSpec(order.shape, lambda n: (0, 0)), w_spec],
        out_specs=[out_spec, out_spec],
        out_shape=[out_shape, out_shape],
        name="project",
        cost_estimate=pl.CostEstimate(flops=600_000_000, bytes_accessed=4_000_000, transcendentals=0),
    )(order, out_weight)


def body(
    queries, key_rows, value_rows, log_decay, write_rate, block_list, attn_gain, delta_gain, out_weight
):
    tokens, packed = queries.shape
    heads = log_decay.shape[1]
    head_dim = packed // heads
    zs, ys, xs = lax.axis_size("z"), lax.axis_size("y"), lax.axis_size("x")
    z_pos, y_pos, core = lax.axis_index("z"), lax.axis_index("y"), lax.axis_index("core")

    kv = jnp.concatenate([key_rows, value_rows], axis=0)

    def hop(value, step):
        return lax.ppermute(value, "z", ring(zs, step))

    def swap(value, axis):
        return lax.all_to_all(value, axis, split_axis=0, concat_axis=0, tiled=True)

    kv_f1, kv_b1 = hop(kv, 1), hop(kv, -1)
    q_arrays = [queries]
    for distance in range(1, ys):
        q_arrays.append(lax.ppermute(queries, "y", ring(ys, distance)))
    listed = block_list.shape[1]
    local_out, emit, ti = delta_local(
        queries,
        key_rows,
        value_rows,
        jnp.transpose(log_decay),
        jnp.transpose(write_rate),
        jnp.transpose(block_list),
    )
    kv_f1, kv_b1, ti = lax.optimization_barrier((kv_f1, kv_b1, ti))
    kv_f2, kv_b2 = hop(kv_f1, 1), hop(kv_b1, -1)
    ti_row = swap(ti, "y")
    lists = ti_row[:, head_dim : head_dim + block_list.shape[0], :listed].astype(jnp.int32)
    groups = row_compose(ti_row, zs)
    groups = swap(groups, "z")
    kv_f3, kv_b3 = hop(kv_f2, 1), hop(kv_b2, -1)
    states = entry_states(z_pos[None].astype(jnp.int32), groups, ti_row)
    states = swap(states, "y")
    kv_f4, kv_b4 = hop(kv_f3[:tokens], 1), hop(kv_b3[tokens:], -1)

    kv_arrays = [kv, kv_f1, kv_f2, kv_f3, kv_f4, kv_b4, kv_b3, kv_b2, kv_b1]
    slots = [0, 2, 4, 6, 8, 9, 10, 12, 14]
    slots = [slot * tokens for slot in slots]
    pos = jnp.stack([z_pos, y_pos]).astype(jnp.int32)
    parts = attend_part(pos, lists, q_arrays, kv_arrays, slots, heads, head_dim, zs)
    arrived = [parts[0]]
    for away in (2, 1, 3):
        arrived.append(lax.ppermute(parts[away], "y", ring(ys, -away)))
    parts = arrived

    model = out_weight.shape[1]
    tile = model // 4
    keep0, send0, order = mix_project(
        core[None].astype(jnp.int32),
        parts,
        local_out,
        emit,
        states,
        attn_gain[None],
        delta_gain[None],
        out_weight,
        xs,
        tile,
        2,
    )
    keep1, send1 = project(order, out_weight, xs, tile, 2, 2)
    x_pos = lax.axis_index("x")
    halves = []
    for keep, send in ((keep0, send0), (keep1, send1)):
        got = lax.ppermute(send, "core", [(0, 1), (1, 0)])
        both = [
            (pick(keep, (x_pos + away) % xs) + pick(got, (x_pos + away) % xs)).astype(BF16)
            for away in range(xs)
        ]
        total = both[0].astype(F32)
        arrived = []
        for away in (2, 1, 3):
            arrived.append(lax.ppermute(both[away], "x", ring(xs, away)))
        for piece in arrived:
            total = total + piece.astype(F32)
        halves.append(total.astype(BF16))
    return jnp.concatenate(halves, axis=1)


def pick(array, index):
    return lax.dynamic_index_in_dim(array, index, axis=0, keepdims=False).astype(F32)


def solution(mesh):
    ys = 4
    cores = 2
    grid = mesh.devices.reshape(
        mesh.shape["heads"] // cores, cores, mesh.shape["ctx"] // ys, ys
    )
    fine = Mesh(grid, ("x", "core", "z", "y"))
    heads, ctx = ("x", "core"), ("z", "y")
    in_specs = (
        P(ctx, heads),
        P(ctx, heads),
        P(ctx, heads),
        P(ctx, heads),
        P(ctx, heads),
        P(ctx, None),
        P(heads),
        P(heads),
        P(heads, None),
    )
    out_specs = P(ctx + heads, None)

    return jax.shard_map(body, mesh=fine, in_specs=in_specs, out_specs=out_specs, check_vma=False)
```
